512 devices in a mesh: ep: 64 (over z, y), tp: 8 (over x, core).
Axes of the slice: x: 4, y: 8, z: 8, core: 2. Of those that a mesh axis runs over, the one named last changes fastest.
Arguments:
- patches: bfloat16 [32768, 1024], P('ep', 'tp'), may hold values from -6 to 6
- patch_grad: bfloat16 [32768, 1024], P('ep', 'tp'), may hold values from -1.796875 to 1.796875
- expert_up: bfloat16 [64, 1024, 4096], P('ep', None, 'tp'), may hold values from -0.1875 to 0.1875
- expert_down: bfloat16 [64, 4096, 1024], P('ep', 'tp'), may hold values from -0.09375 to 0.09375
- expert_counts: int32 [64, 64], P('ep'), may hold values from 1 to 16, as said below
Outputs:
- input_grad: bfloat16 [32768, 1024], P('ep', 'tp')
- up_grad: bfloat16 [64, 1024, 4096], P('ep', None, 'tp')
- down_grad: bfloat16 [64, 4096, 1024], P('ep', 'tp')
The draws below stay inside these ranges and needn't reach their ends.
Inputs may be any that keep to these rules, and one draw needn't show every extreme that they name: `expert_counts`: row s gives, for each of the 64 experts in order, how many of the 512 rows of ep index s are routed to it; those rows stand together in expert order. Every row sums to 512, and one expert has exactly 16 rows from every index of ep.
All inputs are finite; a program needn't handle non-finite values.
Results may differ from the reference program's by a relative error of at most 0.0049.
Values may be sent and summed in bfloat16 or wider, within the bound.
No kernel may reach another device: no remote copies, remote signals or barrier semaphores. Data moves between devices by JAX's collectives and lax.ppermute only.
A program may use at most 64 MiB of HBM per device.

```python
import jax
import jax.numpy as jnp
from jax import lax

D = 1024
H = 4096
TOK_DEV = 512
EXPERTS = 64
CAP = 16
TOKENS = 32768
N_EP = 64


def draw_expert_counts(key, part):
    hot_key = jax.random.fold_in(key, 7)
    hot_expert = jax.random.randint(hot_key, (), 0, EXPERTS).astype(jnp.int32)
    order_key = jax.random.fold_in(key, 11)

    def one_source(source):
        source_key = jax.random.fold_in(order_key, source)
        scores = jax.random.permutation(source_key, EXPERTS * CAP).astype(jnp.int32).reshape(EXPERTS, CAP)
        slot_ids = lax.broadcasted_iota(jnp.int32, (EXPERTS, CAP), 1)
        expert_ids = lax.broadcasted_iota(jnp.int32, (EXPERTS, CAP), 0)
        forced = (slot_ids == 0) | (expert_ids == hot_expert)
        scores = scores + jnp.where(forced, 2 * EXPERTS * CAP, 0).astype(jnp.int32)
        top_values, _ = lax.top_k(scores.reshape(-1), TOK_DEV)
        cutoff = top_values[TOK_DEV - 1]
        chosen = (scores >= cutoff).astype(jnp.int32)
        return jnp.sum(chosen, axis=1).astype(jnp.int32)
    return jax.vmap(one_source)(jnp.arange(N_EP, dtype=jnp.int32))


def block_scale(stream_key, extent, split, least, largest):
    factor_of = 1.0
    for position, shards_of in split:
        steps = jax.random.uniform(jax.random.fold_in(jax.random.fold_in(stream_key, 6), position), (shards_of,), jnp.float32, least / len(split), largest / len(split))
        factor_of = factor_of * jnp.repeat(jnp.exp(steps), extent[position] // shards_of).reshape((-1,) + (1,) * (len(extent) - 1 - position))
    return factor_of


def scatter_about(rng, extent, width, limit, pieces=(), held_as=jnp.bfloat16):
    values = jax.random.normal(rng, extent, jnp.float32) * width
    if len(pieces) > 0:
        values = block_scale(rng, extent, pieces, -0.22, 0.18) * values
    return jnp.clip(values, min=-limit, max=limit).astype(held_as)


def setup_inputs(seed: int = 0) -> dict:
    key_list = jax.random.split(jax.random.key(seed), 6)
    return {
        "patches": scatter_about(key_list[0], (TOKENS, D), 1.0, 6.0, ((0, 64), (1, 8))),
        "patch_grad": scatter_about(key_list[1], (TOKENS, D), 0.3, 1.796875, ((0, 64), (1, 8))),
        "expert_up": scatter_about(key_list[2], (EXPERTS, D, H), D ** -0.5, 0.1875, ((0, 64), (2, 8))),
        "expert_down": scatter_about(key_list[3], (EXPERTS, H, D), H ** -0.5, 0.09375, ((0, 64), (1, 8))),
        "expert_counts": draw_expert_counts(jax.random.fold_in(key_list[5], 71), 0),
    }


def activation(values):
    return jax.nn.gelu(values, approximate=True)

def expert_backward(inputs):
    slot_rows, slot_grads, weight_up, weight_down = inputs
    pre_act = jnp.dot(slot_rows, weight_up, preferred_element_type=jnp.float32)
    act_value, act_back = jax.vjp(activation, pre_act)
    hidden = act_value.astype(jnp.bfloat16)
    hidden_grad = lax.dot_general(slot_grads, weight_down, (((1,), (1,)), ((), ())), preferred_element_type=jnp.float32)
    pre_grad = act_back(hidden_grad)[0].astype(jnp.bfloat16)
    down_part = lax.dot_general(hidden, slot_grads, (((0,), (0,)), ((), ())), preferred_element_type=jnp.float32)
    up_part = lax.dot_general(slot_rows, pre_grad, (((0,), (0,)), ((), ())), preferred_element_type=jnp.float32)
    row_part = lax.dot_general(pre_grad, weight_up, (((1,), (1,)), ((), ())), preferred_element_type=jnp.float32)
    return (up_part.astype(jnp.bfloat16), down_part.astype(jnp.bfloat16), row_part.astype(jnp.bfloat16))

def place_rows(source_table, chosen):
    picked = jnp.take(source_table, chosen.reshape(-1), axis=0)
    return picked.reshape(EXPERTS, CAP, source_table.shape[1])

def take_rows(source_table, chosen):
    return jnp.take(source_table, chosen, axis=0)

def reference(patches, patch_grad, expert_up, expert_down, expert_counts):
    feature_width = patches.shape[1]
    counts_int = expert_counts.astype(jnp.int32)
    row_ends = jnp.cumsum(counts_int, axis=1).astype(jnp.int32)
    row_starts = (row_ends - counts_int).astype(jnp.int32)
    positions = lax.broadcasted_iota(jnp.int32, (N_EP, EXPERTS, CAP), 2)
    slot_live = positions < counts_int[:, :, None]
    slot_source = jnp.where(slot_live, row_starts[:, :, None] + positions, 0).astype(jnp.int32)
    source_rows = patches.reshape(N_EP, TOK_DEV, feature_width)
    source_grads = patch_grad.reshape(N_EP, TOK_DEV, feature_width)
    zero_value = jnp.zeros((), patches.dtype)
    slot_rows = jnp.where(slot_live[..., None], jax.vmap(place_rows)(source_rows, slot_source), zero_value)
    slot_grads = jnp.where(slot_live[..., None], jax.vmap(place_rows)(source_grads, slot_source), zero_value)
    slot_rows = slot_rows.transpose(1, 0, 2, 3).reshape(EXPERTS, N_EP * CAP, feature_width)
    slot_grads = slot_grads.transpose(1, 0, 2, 3).reshape(EXPERTS, N_EP * CAP, feature_width)
    up_grad, down_grad, row_grads = lax.map(expert_backward, (slot_rows, slot_grads, expert_up, expert_down))
    row_grads = row_grads.reshape(EXPERTS, N_EP, CAP, feature_width).transpose(1, 0, 2, 3)
    row_grads = row_grads.reshape(N_EP, EXPERTS * CAP, feature_width)
    row_ids = lax.broadcasted_iota(jnp.int32, (N_EP, TOK_DEV, EXPERTS), 1)
    row_expert = lax.optimization_barrier(jnp.sum((row_ids >= row_ends[:, None, :]).astype(jnp.int32), axis=2)).astype(jnp.int32)
    expert_ids = lax.broadcasted_iota(jnp.int32, (N_EP, TOK_DEV, EXPERTS), 2)
    own_start = lax.optimization_barrier(jnp.sum(jnp.where(row_expert[:, :, None] == expert_ids, row_starts[:, None, :], 0), axis=2)).astype(jnp.int32)
    row_numbers = lax.broadcasted_iota(jnp.int32, (N_EP, TOK_DEV), 1)
    row_slot = (row_expert * CAP + row_numbers - own_start).astype(jnp.int32)
    input_grad = jax.vmap(take_rows)(row_grads, row_slot).reshape(N_EP * TOK_DEV, feature_width)
    return (input_grad, up_grad, down_grad)
```

```python
import jax
import jax.numpy as jnp
from jax import lax
from jax.experimental import pallas as pl
from jax.experimental.pallas import tpu as pltpu
from jax.sharding import Mesh, PartitionSpec as P

F32 = jnp.float32
BF16 = jnp.bfloat16
LANES = 128
ROW_STEPS = 4


def slot_onehot(counts, capacity, row_count):
    experts = counts.shape[1]
    slots = experts * capacity
    slot_ids = lax.broadcasted_iota(jnp.int32, (slots, experts), 0)
    expert_ids = lax.broadcasted_iota(jnp.int32, (slots, experts), 1)
    slot_expert = slot_ids // capacity
    zero = jnp.zeros((), jnp.int32)
    starts = jnp.sum(jnp.where(expert_ids < slot_expert, counts, zero), axis=1, keepdims=True)
    own = jnp.sum(jnp.where(expert_ids == slot_expert, counts, zero), axis=1, keepdims=True)
    position = lax.broadcasted_iota(jnp.int32, (slots, 1), 0) % capacity
    row_of_slot = jnp.where(position < own, starts + position, -1)
    rows = lax.broadcasted_iota(jnp.int32, (slots, row_count), 1)
    return jnp.where(rows == row_of_slot, 1.0, 0.0).astype(BF16)


def fill_kernel(counts_ref, rows_ref, grads_ref, out_ref):
    experts, _, capacity, width = out_ref.shape
    onehot = slot_onehot(counts_ref[...], capacity, rows_ref.shape[0])
    for which, ref in enumerate((rows_ref, grads_ref)):
        picked = jnp.dot(onehot, ref[...], preferred_element_type=F32)
        out_ref[:, which] = picked.astype(BF16).reshape(experts, capacity, width)


def fill_slots(counts, rows, grads, experts, capacity):
    return pl.pallas_call(
        fill_kernel,
        out_shape=jax.ShapeDtypeStruct((experts, 2, capacity, rows.shape[1]), BF16),
        name="fill_slots",
    )(counts, rows, grads)


def unfill_kernel(counts_ref, slots_ref, out_ref):
    experts, capacity, width = slots_ref.shape
    onehot = slot_onehot(counts_ref[...], capacity, out_ref.shape[0])
    table = slots_ref[...].reshape(experts * capacity, width)
    picked = lax.dot_general(onehot, table, (((0,), (0,)), ((), ())), preferred_element_type=F32)
    out_ref[...] = picked.astype(BF16)


def unfill_slots(counts, slots, row_count):
    return pl.pallas_call(
        unfill_kernel,
        out_shape=jax.ShapeDtypeStruct((row_count, slots.shape[2]), BF16),
        name="unfill_slots",
    )(counts, slots)


def expert_kernel(place_ref, own, left, right, far_lo, far_hi, own2, left2, right2, far_lo2, far_hi2,
                  up_ref, down_ref, x_ref, g_ref, hid_ref, pg_ref, theirs_ref, mine_ref, row_scr):
    step = pl.program_id(0)
    steps = pl.num_programs(0)
    at = place_ref[0]
    core = place_ref[1]
    rows = x_ref.shape[0]
    chips = theirs_ref.shape[0]

    def put(ref, shift, which):
        block = lax.rem(at + shift, chips) * 2 + which
        lanes = pl.ds(pl.multiple_of(block * LANES, LANES), LANES)
        x_ref[:, lanes] = ref[:, 0].reshape(rows, LANES)
        g_ref[:, lanes] = ref[:, 1].reshape(rows, LANES)

    for refs, which in (((own, left, right, far_lo, far_hi), core), ((own2, left2, right2, far_lo2, far_hi2), 1 - core)):
        put(refs[0], 0, which)
        put(refs[1], 3, which)
        put(refs[2], 1, which)

        @pl.when(step < steps // 2)
        def _():
            put(refs[3], 2, which)

        @pl.when(step >= steps // 2)
        def _():
            put(refs[4], 2, which)

    up = up_ref[...]
    pre = jnp.dot(x_ref[...], up, preferred_element_type=F32)
    hidden_grad = lax.dot_general(g_ref[...], down_ref[...], (((1,), (1,)), ((), ())), preferred_element_type=F32)
    scale = 0.7978845608028654
    square = pre * pre
    tanh = jnp.tanh(scale * (pre + 0.044715 * (square * pre)))
    half = 0.5 * (1.0 + tanh)
    hid_ref[...] = (pre * half).astype(BF16)
    slope = half + 0.5 * pre * (1.0 - tanh * tanh) * (scale * (1.0 + (3.0 * 0.044715) * square))
    pre_grad = (hidden_grad * slope).astype(BF16)
    pg_ref[...] = pre_grad
    row_scr[...] = lax.dot_general(pre_grad, up, (((1,), (1,)), ((), ())), preferred_element_type=F32)
    for chip in range(chips):
        own_lanes = pl.ds(pl.multiple_of((2 * chip + core) * LANES, LANES), LANES)
        their_lanes = pl.ds(pl.multiple_of((2 * chip + 1 - core) * LANES, LANES), LANES)
        mine_ref[chip] = row_scr[:, own_lanes]
        theirs_ref[chip] = row_scr[:, their_lanes].astype(BF16)


def expert_compute(place, pieces, pieces2, up, down):
    own = pieces[0]
    sources, _, capacity, _ = own.shape
    slots = sources * capacity
    width, hidden = up.shape
    part = sources // ROW_STEPS
    rows = part * capacity
    half_steps = ROW_STEPS // 2
    block = (part, 2, capacity, LANES)
    whole = pl.BlockSpec(block, lambda i: (i, 0, 0, 0))
    low = pl.BlockSpec(block, lambda i: (jnp.minimum(i, half_steps - 1), 0, 0, 0))
    high = pl.BlockSpec(block, lambda i: (jnp.maximum(i - half_steps, 0), 0, 0, 0))
    chunk_specs = [whole, whole, whole, low, high]
    row_block = lambda n: pl.BlockSpec((rows, n), lambda i: (i, 0))
    chip_block = pl.BlockSpec((width // (2 * LANES), rows, LANES), lambda i: (0, i, 0))
    chips = width // (2 * LANES)
    return pl.pallas_call(
        expert_kernel,
        grid=(ROW_STEPS,),
        in_specs=[pl.BlockSpec(memory_space=pltpu.SMEM)] + chunk_specs * 2 + [
            pl.BlockSpec(up.shape, lambda i: (0, 0)),
            pl.BlockSpec(down.shape, lambda i: (0, 0)),
        ],
        out_specs=[row_block(width), row_block(width), row_block(hidden), row_block(hidden), chip_block, chip_block],
        out_shape=[
            jax.ShapeDtypeStruct((slots, width), BF16),
            jax.ShapeDtypeStruct((slots, width), BF16),
            jax.ShapeDtypeStruct((slots, hidden), BF16),
            jax.ShapeDtypeStruct((slots, hidden), BF16),
            jax.ShapeDtypeStruct((chips, slots, LANES), BF16),
            jax.ShapeDtypeStruct((chips, slots, LANES), F32),
        ],
        scratch_shapes=[pltpu.VMEM((rows, width), F32)],
        name="expert_compute",
    )(place, *pieces, *pieces2, up, down)


def to_right(value):
    return lax.ppermute(value, "x", [(i, (i + 1) % 4) for i in range(4)])


def to_left(value):
    return lax.ppermute(value, "x", [(i, (i - 1) % 4) for i in range(4)])


def to_other_core(value):
    return lax.ppermute(value, "core", [(0, 1), (1, 0)])


def per_device(patches, patch_grad, expert_up, expert_down, expert_counts):
    row_count = patches.shape[0]
    experts = expert_counts.shape[1]
    capacity = 2 * row_count // experts
    up = expert_up[0]
    down = expert_down[0]
    place = jnp.stack([lax.axis_index("x"), lax.axis_index("core")]).astype(jnp.int32)
    send = fill_slots(expert_counts, patches, patch_grad, experts, capacity)
    own = lax.all_to_all(send, "ep", split_axis=0, concat_axis=0, tiled=True)
    left = to_right(own)
    right = to_left(own)
    half = own.shape[0] // 2
    far_lo = to_right(left[:half])
    far_hi = to_left(right[half:])
    pieces = (own, left, right, far_lo, far_hi)
    pieces2 = tuple(to_other_core(piece) for piece in pieces)
    slot_rows, slot_grads, hidden, pre_grad, theirs, mine = expert_compute(place, pieces, pieces2, up, down)
    chip_sum = (mine + to_other_core(theirs).astype(F32)).astype(BF16)
    parts = lax.all_to_all(chip_sum, "x", split_axis=0, concat_axis=0, tiled=True)
    wide = parts.astype(F32)
    summed = ((wide[0] + wide[1]) + (wide[2] + wide[3])).astype(BF16)
    back = summed.reshape(experts, capacity, summed.shape[1])
    returned = lax.all_to_all(back, "ep", split_axis=0, concat_axis=0, tiled=True)
    down_part = lax.dot_general(hidden, slot_grads, (((0,), (0,)), ((), ())), preferred_element_type=F32)
    up_part = lax.dot_general(slot_rows, pre_grad, (((0,), (0,)), ((), ())), preferred_element_type=F32)
    input_grad = unfill_slots(expert_counts, returned, row_count)
    return (input_grad, up_part.astype(BF16)[None], down_part.astype(BF16)[None])


def solution(mesh):
    fine = Mesh(mesh.devices.reshape(mesh.shape["ep"], mesh.shape["tp"] // 2, 2), ("ep", "x", "core"))
    tp = ("x", "core")
    return jax.shard_map(
        per_device,
        mesh=fine,
        in_specs=(P("ep", tp), P("ep", tp), P("ep", None, tp), P("ep", tp, None), P("ep", None)),
        out_specs=(P("ep", tp), P("ep", None, tp), P("ep", tp, None)),
        check_vma=False,
    )
```
